256 devices in a mesh: gx: 8 (over z), gy: 32 (over y, x, core).
Axes of the slice: x: 4, y: 4, z: 8, core: 2. Of those that a mesh axis runs over, the one named last changes fastest.
Arguments:
- ocean_field: float32 [16, 1024, 4096], P(None, 'gx', 'gy'), may hold values from -6 to 6
Outputs:
- detail_one: float32 [7, 8, 512, 2048], P(None, None, 'gx', 'gy')
- detail_two: float32 [7, 4, 256, 1024], P(None, None, 'gx', 'gy')
- detail_three: float32 [7, 2, 128, 512], P(None, None, 'gx', 'gy')
- approximation: float32 [2, 128, 512], P(None, 'gx', 'gy')
The draws below stay inside these ranges and needn't reach their ends.
All inputs are finite; a program needn't handle non-finite values.
Results may differ from the reference program's by a relative error of at most 0.000022.
Values sent between devices are 32-bit elements; how exact they have to be, the bound alone decides.
A program may use at most 64 MiB of HBM per device.

```python
import jax
import jax.numpy as jnp
from jax import lax

DEPTH = 16
NX = 1024
NY = 4096


def block_levels(key, extent, pieces, low, largest):
    factor_of, own = 1.0, jax.random.fold_in(key, 6)
    for axis_at, parts in pieces:
        steps = jnp.exp(jax.random.uniform(jax.random.fold_in(own, axis_at), (parts,), jnp.float32, low / len(pieces), largest / len(pieces)))
        factor_of = factor_of * jnp.repeat(steps, extent[axis_at] // parts).reshape([-1 if axis == axis_at else 1 for axis in range(len(extent))])
    return factor_of


def bell_draw(rng, shape, scale, limit, shards=(), kind=jnp.bfloat16):
    values = scale * jax.random.normal(rng, shape, jnp.float32)
    if shards:
        values = values * block_levels(rng, shape, shards, -0.22, 0.18)
    return jnp.clip(values, -limit, limit).astype(kind)


def setup_inputs(seed: int = 0) -> dict:
    seeds = jax.random.split(jax.random.key(seed), 2)
    return {
        "ocean_field": bell_draw(seeds[0], (DEPTH, NX, NY), 1.0, 6.0, ((1, 8), (2, 32)), jnp.float32),
    }


LIFT_ALPHA = -1.586134342
LIFT_BETA = -0.05298011854
LIFT_GAMMA = 0.8829110762
LIFT_DELTA = 0.4435068522
LIFT_SCALE = 1.149604398
LIFT_INVERSE = 0.869864452


def split_pairs(blocks, axis_dim):
    shape = blocks.shape
    paired = blocks.reshape(shape[:axis_dim] + (shape[axis_dim] // 2, 2) + shape[axis_dim + 1:])
    return lax.index_in_dim(paired, 0, axis_dim + 1, False), lax.index_in_dim(paired, 1, axis_dim + 1, False)


def lift_axis(blocks, axis_dim, next_even, prior_odd):
    even_part, odd_part = split_pairs(blocks, axis_dim)
    odd_part = odd_part + LIFT_ALPHA * (even_part + next_even(even_part))
    even_part = even_part + LIFT_BETA * (prior_odd(odd_part) + odd_part)
    odd_part = odd_part + LIFT_GAMMA * (even_part + next_even(even_part))
    even_part = even_part + LIFT_DELTA * (prior_odd(odd_part) + odd_part)
    stacked = jnp.stack([even_part * LIFT_SCALE, odd_part * LIFT_INVERSE])
    return stacked.reshape((2 * blocks.shape[0],) + stacked.shape[2:])


def mirror_lift(blocks):
    def next_even(values):
        return jnp.concatenate([values[:, 1:], values[:, -1:]], axis=1)

    def prior_odd(values):
        return jnp.concatenate([values[:, :1], values[:, :-1]], axis=1)

    return lift_axis(blocks, 1, next_even, prior_odd)


def wrap_lift(blocks, axis_dim):
    def next_even(values):
        return jnp.roll(values, -1, axis=axis_dim)

    def prior_odd(values):
        return jnp.roll(values, 1, axis=axis_dim)

    return lift_axis(blocks, axis_dim, next_even, prior_odd)


def one_level(blocks):
    blocks = wrap_lift(blocks, 2)
    blocks = wrap_lift(blocks, 3)
    return mirror_lift(blocks)


def reference(ocean_field):
    blocks = one_level(ocean_field[None])
    detail_one = blocks[1:]
    blocks = one_level(blocks[:1])
    detail_two = blocks[1:]
    blocks = one_level(blocks[:1])
    detail_three = blocks[1:]
    return detail_one, detail_two, detail_three, blocks[0]
```

```python
import functools

import jax
import jax.numpy as jnp
import numpy as np
from jax import lax
from jax.experimental import pallas as pl
from jax.experimental.pallas import tpu as pltpu
from jax.sharding import PartitionSpec as P

LIFT_ALPHA = -1.586134342
LIFT_BETA = -0.05298011854
LIFT_GAMMA = 0.8829110762
LIFT_DELTA = 0.4435068522
LIFT_SCALE = 1.149604398
LIFT_INVERSE = 0.869864452

MESH = pl.DeviceIdType.MESH
N = 128
TOP = 32
EXT = 192
LEFT, RIGHT, HIGH, PLANES = 8, 11, 14, 22
DEEP = 13


def lift_matrix(extent):
    v = np.eye(extent)
    s, d = v[0::2], v[1::2]
    d = d + LIFT_ALPHA * (s + np.roll(s, -1, 0))
    s = s + LIFT_BETA * (np.roll(d, 1, 0) + d)
    d = d + LIFT_GAMMA * (s + np.roll(s, -1, 0))
    s = s + LIFT_DELTA * (np.roll(d, 1, 0) + d)
    return LIFT_SCALE * s, LIFT_INVERSE * d


def lane_filters():
    low1, high1 = lift_matrix(2 * N)
    low2, high2 = lift_matrix(N)
    low3, high3 = lift_matrix(N // 2)
    one = np.concatenate([low1[: N // 2], high1[: N // 2]]).T
    two = np.concatenate([(low2 @ low1)[: N // 4], (high2 @ low1)[: N // 4]]).T
    three = np.concatenate([(low3 @ low2 @ low1)[: N // 8], (high3 @ low2 @ low1)[: N // 8]]).T
    pad = lambda w: np.pad(w, ((0, 0), (0, N - w.shape[1]))).astype(np.float32)
    return np.stack([pad(one), pad(two), pad(three)])


def mirror_lift(planes):
    count = len(planes) // 2
    s, d = list(planes[0::2]), list(planes[1::2])
    after = lambda v, n: v[min(n + 1, count - 1)]
    before = lambda v, n: v[max(n - 1, 0)]
    d = [d[n] + LIFT_ALPHA * (s[n] + after(s, n)) for n in range(count)]
    s = [s[n] + LIFT_BETA * (before(d, n) + d[n]) for n in range(count)]
    d = [d[n] + LIFT_GAMMA * (s[n] + after(s, n)) for n in range(count)]
    s = [s[n] + LIFT_DELTA * (before(d, n) + d[n]) for n in range(count)]
    return [v * LIFT_SCALE for v in s], [v * LIFT_INVERSE for v in d]


def row_lift(s, d):
    rows = s.shape[0]
    after = lambda v: pltpu.roll(v, rows - 1, 0)
    before = lambda v: pltpu.roll(v, 1, 0)
    d = d + LIFT_ALPHA * (s + after(s))
    s = s + LIFT_BETA * (before(d) + d)
    d = d + LIFT_GAMMA * (s + after(s))
    s = s + LIFT_DELTA * (before(d) + d)
    return s * LIFT_SCALE, d * LIFT_INVERSE


def exchange_kernel(x_ref, z_ref, field, strips, load_sem, send_sem, recv_sem):
    nx, ny = lax.axis_size("gx"), lax.axis_size("gy")
    gx, gy = lax.axis_index("gx"), lax.axis_index("gy")
    up, down = lax.rem(gx + nx - 1, nx), lax.rem(gx + 1, nx)
    left, right = lax.rem(gy + ny - 1, ny), lax.rem(gy + 1, ny)
    barrier = pltpu.get_barrier_semaphore()
    around = [(up, gy), (down, gy), (gx, left), (gx, right), (up, left), (up, right), (down, left), (down, right)]
    for device in around:
        pl.semaphore_signal(barrier, inc=1, device_id=device, device_id_type=MESH)

    chunk = N // 4
    loads = []
    for c in range(4):
        rows = pl.ds(c * chunk, chunk)
        loads.append(pltpu.make_async_copy(x_ref.at[:, rows], field.at[:, rows], load_sem.at[c]))
        loads[-1].start()
    lane = lax.broadcasted_iota(jnp.int32, (8, N), 1)

    def block(i, _):
        at = pl.multiple_of(i * 8, 8)
        low, high = mirror_lift([field[z, pl.ds(at, 8), :] for z in range(16)])
        own = pl.ds(at + TOP, 8)
        for n in range(8):
            z_ref[n, own, :] = low[n]
            z_ref[HIGH + n, own, :] = high[n]
        here = pl.ds(at, 8)
        for g in range(3):
            group = [low[:4], low[4:], high][g]
            count = len(group)
            wide = N // count
            to_right, to_left = None, None
            for j in range(count):
                shift = wide * (j + 1) % N
                turned = pltpu.roll(group[j], shift, 1) if shift else group[j]
                slot = lane // wide
                to_right = turned if j == 0 else jnp.where(slot == j, turned, to_right)
                to_left = turned if j == 0 else jnp.where(slot == (j + 1) % count, turned, to_left)
            strips[g, here, :] = to_right
            strips[3 + g, here, :] = to_left
        return 0

    for c in range(4):
        loads[c].wait()
        lax.fori_loop(c * 4, c * 4 + 4, block, 0)

    pl.semaphore_wait(barrier, len(around))
    low, high = pl.ds(0, 8), pl.ds(HIGH, 8)
    lefts, rights = pl.ds(LEFT, 3), pl.ds(RIGHT, 3)
    to_right, to_left = pl.ds(0, 3), pl.ds(3, 3)
    own = pl.ds(TOP, N)
    head, tail = pl.ds(0, 24), pl.ds(N - 32, 32)
    above, below = pl.ds(0, 32), pl.ds(TOP + N, 24)
    moves = [
        (z_ref.at[low, pl.ds(TOP + N - 32, 32)], z_ref.at[low, above], (down, gy)),
        (z_ref.at[low, pl.ds(TOP, 24)], z_ref.at[low, below], (up, gy)),
        (z_ref.at[high, pl.ds(TOP + N - 8, 8)], z_ref.at[high, pl.ds(TOP - 8, 8)], (down, gy)),
        (z_ref.at[high, pl.ds(TOP, 8)], z_ref.at[high, pl.ds(TOP + N, 8)], (up, gy)),
        (strips.at[to_right], z_ref.at[lefts, own], (gx, right)),
        (strips.at[to_left], z_ref.at[rights, own], (gx, left)),
        (strips.at[to_right, tail], z_ref.at[lefts, above], (down, right)),
        (strips.at[to_right, head], z_ref.at[lefts, below], (up, right)),
        (strips.at[to_left, tail], z_ref.at[rights, above], (down, left)),
        (strips.at[to_left, head], z_ref.at[rights, below], (up, left)),
    ]
    copies = []
    for k, (source, target, device) in enumerate(moves):
        copies.append(
            pltpu.make_async_remote_copy(
                src_ref=source,
                dst_ref=target,
                send_sem=send_sem.at[k],
                recv_sem=recv_sem.at[k],
                device_id=device,
                device_id_type=MESH,
            )
        )
        copies[-1].start()
    for copy in copies:
        copy.wait_recv()
    for copy in copies:
        copy.wait_send()


def exchange(field):
    return pl.pallas_call(
        exchange_kernel,
        out_shape=jax.ShapeDtypeStruct((PLANES, EXT, N), jnp.float32),
        in_specs=[pl.BlockSpec(memory_space=pl.ANY)],
        out_specs=pl.BlockSpec(memory_space=pltpu.VMEM),
        scratch_shapes=[
            pltpu.VMEM((16, N, N), jnp.float32),
            pltpu.VMEM((6, N, N), jnp.float32),
            pltpu.SemaphoreType.DMA((4,)),
            pltpu.SemaphoreType.DMA((10,)),
            pltpu.SemaphoreType.DMA((10,)),
        ],
        compiler_params=pltpu.CompilerParams(collective_id=0, has_side_effects=True, vmem_limit_bytes=16 << 20),
        name="exchange",
    )(field)


def transform_kernel(z_ref, w_ref, one_ref, two_ref, three_ref, last_ref, r1, z2, r2, z3, r3, y2, y3):
    half, quarter, eighth = N // 2, N // 4, N // 8

    def first(p, _):
        s, d = row_lift(z_ref[p, pl.ds(0, EXT // 2, stride=2), :], z_ref[p, pl.ds(1, EXT // 2, stride=2), :])
        z2[p] = s
        r1[p, pl.ds(0, half), :] = s[TOP // 2 : TOP // 2 + half]
        r1[p, pl.ds(half, half), :] = d[TOP // 2 : TOP // 2 + half]
        return 0

    def later(p, _):
        s, d = row_lift(z2[p, pl.ds(0, EXT // 4, stride=2), :], z2[p, pl.ds(1, EXT // 4, stride=2), :])
        z3[p] = s
        r2[p, pl.ds(0, quarter), :] = s[TOP // 4 : TOP // 4 + quarter]
        r2[p, pl.ds(quarter, quarter), :] = d[TOP // 4 : TOP // 4 + quarter]
        s, d = row_lift(z3[p, pl.ds(0, EXT // 8, stride=2), :], z3[p, pl.ds(1, EXT // 8, stride=2), :])
        r3[p, pl.ds(0, eighth), :] = s[TOP // 8 : TOP // 8 + eighth]
        r3[p, pl.ds(eighth, eighth), :] = d[TOP // 8 : TOP // 8 + eighth]
        return 0

    lax.fori_loop(0, PLANES, first, 0)
    lax.fori_loop(0, DEEP, later, 0)

    def along_y(r, plane, group, slot, count, level):
        wide = N // count
        lane = lax.broadcasted_iota(jnp.int32, r.shape[1:], 1)
        halo = jnp.where(lane // wide == slot, r[LEFT + group], r[RIGHT + group])
        shift = lax.rem(2 * N - wide * (slot + 1), N)
        halo = pltpu.roll(halo, shift, 1)
        return jnp.dot(
            jnp.concatenate([r[plane], halo], axis=1),
            w_ref[level],
            precision=lax.Precision.HIGHEST,
            preferred_element_type=jnp.float32,
        )

    def low_planes(p, _):
        group, slot = p // 4, lax.rem(p, 4)
        out = along_y(r1, p, group, slot, 4, 0)
        one_ref[0, p] = out[half:, :half]
        one_ref[1, p] = out[:half, half:]
        one_ref[2, p] = out[half:, half:]
        y2[p] = along_y(r2, p, group, slot, 4, 1)
        y3[p] = along_y(r3, p, group, slot, 4, 2)
        return 0

    def high_planes(q, _):
        out = along_y(r1, HIGH + q, 2, q, 8, 0)
        one_ref[3, q] = out[:half, :half]
        one_ref[4, q] = out[half:, :half]
        one_ref[5, q] = out[:half, half:]
        one_ref[6, q] = out[half:, half:]
        return 0

    lax.fori_loop(0, 8, low_planes, 0)
    lax.fori_loop(0, 8, high_planes, 0)

    def put(ref, last, low, high, size):
        for n in range(len(low)):
            for band, planes in ((0, low), (4, high)):
                v = planes[n]
                for j in range(4):
                    by, bx = j // 2, j % 2
                    part = v[bx * size : (bx + 1) * size, by * size : (by + 1) * size]
                    if band + j:
                        ref[band + j - 1, n] = part
                    elif last is not None:
                        last[n] = part

    low, high = mirror_lift([y2[p] for p in range(8)])
    put(two_ref, None, low, high, quarter)
    low, _ = mirror_lift([y3[p] for p in range(8)])
    low, high = mirror_lift(low)
    put(three_ref, last_ref, low, high, eighth)


def transform(extended, filters):
    f32 = jnp.float32
    vmem = pl.BlockSpec(memory_space=pltpu.VMEM)
    return pl.pallas_call(
        transform_kernel,
        out_shape=(
            jax.ShapeDtypeStruct((7, 8, N // 2, N // 2), f32),
            jax.ShapeDtypeStruct((7, 4, N // 4, N // 4), f32),
            jax.ShapeDtypeStruct((7, 2, N // 8, N // 8), f32),
            jax.ShapeDtypeStruct((2, N // 8, N // 8), f32),
        ),
        in_specs=[vmem, vmem],
        out_specs=(vmem,) * 4,
        scratch_shapes=[
            pltpu.VMEM((PLANES, N, N), f32),
            pltpu.VMEM((PLANES, EXT // 2, N), f32),
            pltpu.VMEM((DEEP, N // 2, N), f32),
            pltpu.VMEM((DEEP, EXT // 4, N), f32),
            pltpu.VMEM((DEEP, N // 4, N), f32),
            pltpu.VMEM((8, N // 2, N), f32),
            pltpu.VMEM((8, N // 4, N), f32),
        ],
        compiler_params=pltpu.CompilerParams(vmem_limit_bytes=24 << 20),
        name="transform",
    )(extended, filters)


def shards(ocean_field):
    return transform(exchange(ocean_field), jnp.asarray(lane_filters()))


def solution(mesh):
    return jax.shard_map(
        shards,
        mesh=mesh,
        in_specs=(P(None, "gx", "gy"),),
        out_specs=(
            P(None, None, "gx", "gy"),
            P(None, None, "gx", "gy"),
            P(None, None, "gx", "gy"),
            P(None, "gx", "gy"),
        ),
        check_vma=False,
    )
```

```python
import functools

import jax
import jax.numpy as jnp
import ml_dtypes
import numpy as np
from jax import lax
from jax.experimental import pallas as pl
from jax.experimental.pallas import tpu as pltpu
from jax.sharding import PartitionSpec as P

LIFT_ALPHA = -1.586134342
LIFT_BETA = -0.05298011854
LIFT_GAMMA = 0.8829110762
LIFT_DELTA = 0.4435068522
LIFT_SCALE = 1.149604398
LIFT_INVERSE = 0.869864452

MESH = pl.DeviceIdType.MESH
N = 128
TOP = 32
EXT = 192
LEFT, RIGHT, HIGH, PLANES = 8, 11, 14, 22
OWN, OWN_DEEP, HALO_DEEP, STRIPS = 0, 1, 2, 3
PAD = 16
DEEP = [0, 1, 2, 3, 4, 5, 6, 7, 8, 9, 11, 12]


def lift_matrix(extent):
    v = np.eye(extent)
    s, d = v[0::2], v[1::2]
    d = d + LIFT_ALPHA * (s + np.roll(s, -1, 0))
    s = s + LIFT_BETA * (np.roll(d, 1, 0) + d)
    d = d + LIFT_GAMMA * (s + np.roll(s, -1, 0))
    s = s + LIFT_DELTA * (np.roll(d, 1, 0) + d)
    return LIFT_SCALE * s, LIFT_INVERSE * d


def lane_filters():
    low1, high1 = lift_matrix(2 * N)
    low2, high2 = lift_matrix(N)
    low3, high3 = lift_matrix(N // 2)
    one = np.concatenate([low1[: N // 2], high1[: N // 2]]).T
    two = np.concatenate([(low2 @ low1)[: N // 4], (high2 @ low1)[: N // 4]]).T
    three = np.concatenate([(low3 @ low2 @ low1)[: N // 8], (high3 @ low2 @ low1)[: N // 8]]).T
    return one, np.concatenate([two, three, np.zeros((2 * N, N // 4))], axis=1)


def strip_filters(one):
    out = np.zeros((6, N, N))
    for plane in range(16):
        group, count = (plane // 4, 4) if plane < 8 else (2, 8)
        slot, wide = plane % count, N // count
        for near in range(wide):
            for k, column in enumerate((126, 127, 0, 1)):
                out[group, slot * wide + near, 4 * plane + k] = one[2 * N - wide + near, column]
                out[3 + group, (slot + 1) % count * wide + near, 4 * plane + k] = one[N + near, column]
            for k, column in enumerate((62, 63, 64)):
                out[group, slot * wide + near, 64 + 4 * plane + k] = one[2 * N - wide + near, column]
                out[3 + group, (slot + 1) % count * wide + near, 64 + 4 * plane + k] = one[N + near, column]
    return out


def parts(values, kind):
    high = values.astype(kind)
    rest = values - high.astype(values.dtype)
    middle = rest.astype(kind)
    return high, middle, (rest - middle.astype(values.dtype)).astype(kind)


def paired(weights):
    high, middle, low = parts(weights, ml_dtypes.bfloat16)
    first = np.concatenate([np.concatenate([high, middle], -1), np.concatenate([middle, high], -1)], -2)
    return first, np.concatenate([low, high], -2)


def product(values, first, second):
    high, middle, low = parts(values, jnp.bfloat16)
    wide = jnp.dot(jnp.concatenate([high, middle], axis=1), first, preferred_element_type=jnp.float32)
    rest = jnp.dot(jnp.concatenate([high, low], axis=1), second, preferred_element_type=jnp.float32)
    return wide[:, :N] + (wide[:, N:] + rest)


def mirror_lift(planes):
    count = len(planes) // 2
    s, d = list(planes[0::2]), list(planes[1::2])
    after = lambda v, n: v[min(n + 1, count - 1)]
    before = lambda v, n: v[max(n - 1, 0)]
    d = [d[n] + LIFT_ALPHA * (s[n] + after(s, n)) for n in range(count)]
    s = [s[n] + LIFT_BETA * (before(d, n) + d[n]) for n in range(count)]
    d = [d[n] + LIFT_GAMMA * (s[n] + after(s, n)) for n in range(count)]
    s = [s[n] + LIFT_DELTA * (before(d, n) + d[n]) for n in range(count)]
    return [v * LIFT_SCALE for v in s], [v * LIFT_INVERSE for v in d]


def row_lift(s, d):
    rows = s.shape[0]
    after = lambda v: pltpu.roll(v, rows - 1, 0)
    before = lambda v: pltpu.roll(v, 1, 0)
    d = d + LIFT_ALPHA * (s + after(s))
    s = s + LIFT_BETA * (before(d) + d)
    d = d + LIFT_GAMMA * (s + after(s))
    s = s + LIFT_DELTA * (before(d) + d)
    return s * LIFT_SCALE, d * LIFT_INVERSE


def exchange_kernel(
    x_ref, first_ref, second_ref, z_ref, own_ref, first, second, field, strips, padded, load_sem, send_sem, recv_sem
):
    nx, ny = lax.axis_size("gx"), lax.axis_size("gy")
    gx, gy = lax.axis_index("gx"), lax.axis_index("gy")
    up, down = lax.rem(gx + nx - 1, nx), lax.rem(gx + 1, nx)
    left, right = lax.rem(gy + ny - 1, ny), lax.rem(gy + 1, ny)
    barrier = pltpu.get_barrier_semaphore()
    around = [(up, gy), (down, gy), (gx, left), (gx, right), (up, left), (up, right), (down, left), (down, right)]
    for device in around:
        pl.semaphore_signal(barrier, inc=1, device_id=device, device_id_type=MESH)

    chunk = N // 4
    loads = []
    for c in range(4):
        rows = pl.ds(c * chunk, chunk)
        loads.append(pltpu.make_async_copy(x_ref.at[:, rows], field.at[:, rows], load_sem.at[c]))
        loads[-1].start()
    weights = [
        pltpu.make_async_copy(first_ref, first, load_sem.at[4]),
        pltpu.make_async_copy(second_ref, second, load_sem.at[5]),
    ]
    for copy in weights:
        copy.start()
    lane = lax.broadcasted_iota(jnp.int32, (8, N), 1)

    def block(i, _):
        at = pl.multiple_of(i * 8, 8)
        low, high = mirror_lift([field[z, pl.ds(at, 8), :] for z in range(16)])
        own = pl.ds(at + TOP, 8)
        for n in range(8):
            z_ref[n, own, :] = low[n]
            z_ref[HIGH + n, own, :] = high[n]
            padded[n, pl.ds(at + PAD, 8), :] = low[n]
            padded[8 + n, pl.ds(at + PAD, 8), :] = high[n]
        here = pl.ds(at, 8)
        for g in range(3):
            group = [low[:4], low[4:], high][g]
            count = len(group)
            wide = N // count
            to_right, to_left = None, None
            for j in range(count):
                shift = wide * (j + 1) % N
                turned = pltpu.roll(group[j], shift, 1) if shift else group[j]
                slot = lane // wide
                to_right = turned if j == 0 else jnp.where(slot == j, turned, to_right)
                to_left = turned if j == 0 else jnp.where(slot == (j + 1) % count, turned, to_left)
            strips[g, here, :] = to_right
            strips[3 + g, here, :] = to_left
        return 0

    for c in range(4):
        loads[c].wait()
        lax.fori_loop(c * 4, c * 4 + 4, block, 0)

    pl.semaphore_wait(barrier, len(around))
    low, high = pl.ds(0, 8), pl.ds(HIGH, 8)
    lefts, rights = pl.ds(LEFT, 3), pl.ds(RIGHT, 3)
    to_right, to_left = pl.ds(0, 3), pl.ds(3, 3)
    own = pl.ds(TOP, N)
    head, tail = pl.ds(0, 24), pl.ds(N - 32, 32)
    above, below = pl.ds(0, 32), pl.ds(TOP + N, 24)
    moves = [
        (z_ref.at[low, pl.ds(TOP + N - 32, 32)], z_ref.at[low, above], (down, gy)),
        (z_ref.at[low, pl.ds(TOP, 24)], z_ref.at[low, below], (up, gy)),
        (z_ref.at[high, pl.ds(TOP + N - 8, 8)], z_ref.at[high, pl.ds(TOP - 8, 8)], (down, gy)),
        (z_ref.at[high, pl.ds(TOP, 8)], z_ref.at[high, pl.ds(TOP + N, 8)], (up, gy)),
        (strips.at[to_right], z_ref.at[lefts, own], (gx, right)),
        (strips.at[to_left], z_ref.at[rights, own], (gx, left)),
        (strips.at[to_right, tail], z_ref.at[lefts, above], (down, right)),
        (strips.at[to_right, head], z_ref.at[lefts, below], (up, right)),
        (strips.at[to_left, tail], z_ref.at[rights, above], (down, left)),
        (strips.at[to_left, head], z_ref.at[rights, below], (up, left)),
    ]
    copies = []
    for k, (source, target, device) in enumerate(moves):
        copies.append(
            pltpu.make_async_remote_copy(
                src_ref=source,
                dst_ref=target,
                send_sem=send_sem.at[k],
                recv_sem=recv_sem.at[k],
                device_id=device,
                device_id_type=MESH,
            )
        )
        copies[-1].start()

    for copy in weights:
        copy.wait()
    padded[:, pl.ds(0, PAD), :] = jnp.zeros((16, PAD, N), jnp.float32)
    padded[:, pl.ds(PAD + N, PAD), :] = jnp.zeros((16, PAD, N), jnp.float32)

    def plane(p, _):
        s, d = row_lift(
            padded[p, pl.ds(0, PAD + N // 2, stride=2), :], padded[p, pl.ds(1, PAD + N // 2, stride=2), :]
        )
        rows = jnp.concatenate([s[PAD // 2 : PAD // 2 + N // 2], d[PAD // 2 : PAD // 2 + N // 2]])
        own_ref[p] = product(rows, first[0], second[0])
        return 0

    lax.fori_loop(0, 16, plane, 0)
    for copy in copies:
        copy.wait_recv()
    for copy in copies:
        copy.wait_send()


def exchange(field, first, second):
    f32 = jnp.float32
    return pl.pallas_call(
        exchange_kernel,
        out_shape=(
            jax.ShapeDtypeStruct((PLANES, EXT, N), f32),
            jax.ShapeDtypeStruct((16, N, N), f32),
            jax.ShapeDtypeStruct(first.shape, first.dtype),
            jax.ShapeDtypeStruct(second.shape, second.dtype),
        ),
        in_specs=[pl.BlockSpec(memory_space=pltpu.HBM)] * 3,
        out_specs=(pl.BlockSpec(memory_space=pltpu.VMEM),) * 4,
        scratch_shapes=[
            pltpu.VMEM((16, N, N), f32),
            pltpu.VMEM((6, N, N), f32),
            pltpu.VMEM((16, N + 2 * PAD, N), f32),
            pltpu.SemaphoreType.DMA((6,)),
            pltpu.SemaphoreType.DMA((10,)),
            pltpu.SemaphoreType.DMA((10,)),
        ],
        compiler_params=pltpu.CompilerParams(collective_id=0, has_side_effects=True, vmem_limit_bytes=20 << 20),
        name="exchange",
    )(*[pltpu.with_memory_space_constraint(v, pltpu.HBM) for v in (field, first, second)])


def transform_kernel(
    z_ref, own_ref, first, second,
    one_ref, two_ref, three_ref, last_ref, one, two, three, last, edge, fix, z2, z3, strip, deep, sem,
):
    half, quarter, eighth = N // 2, N // 4, N // 8
    sub = lax.broadcasted_iota(jnp.int32, (8, N), 0)
    lane = lax.broadcasted_iota(jnp.int32, (8, N), 1)
    zero = jnp.zeros((8, N), jnp.float32)

    for p in range(16):
        q = p if p < 8 else HIGH + p - 8
        edge[0, pl.ds(16 * p, 8), :] = z_ref[q, pl.ds(TOP - 8, 8), :]
        edge[0, pl.ds(16 * p + 8, 8), :] = zero
        edge[1, pl.ds(16 * p, 8), :] = zero
        edge[1, pl.ds(16 * p + 8, 8), :] = z_ref[q, pl.ds(TOP + N, 8), :]
    rows = []
    for t, shift in ((0, N - 4), (1, 4)):
        pair = row_lift(edge[t, pl.ds(0, N, stride=2), :], edge[t, pl.ds(1, N, stride=2), :])
        rows.append([pltpu.roll(v, shift, 0) for v in pair])
    place = lax.rem(lax.broadcasted_iota(jnp.int32, (N, N), 0), 8)
    for bx in range(2):
        both = jnp.where(place < 2 - bx, rows[0][bx], jnp.where(place >= 6, rows[1][bx], 0.0))
        fix[bx] = product(both, first[OWN], second[OWN])

    for p in range(14):
        s, d = row_lift(z_ref[p, pl.ds(0, EXT // 2, stride=2), :], z_ref[p, pl.ds(1, EXT // 2, stride=2), :])
        if p in DEEP:
            z2[p] = s
        if p >= LEFT:
            strip[p - LEFT, pl.ds(0, half), :] = s[TOP // 2 : TOP // 2 + half]
            strip[p - LEFT, pl.ds(half, half), :] = d[TOP // 2 : TOP // 2 + half]
    total = product(strip[0], first[STRIPS], second[STRIPS])
    for t in range(1, 6):
        total = total + product(strip[t], first[STRIPS + t], second[STRIPS + t])
    strip[0] = total

    reached = (lane < 2) | (lane >= N - 2) | ((lane >= half - 2) & (lane <= half))

    def level_one(p, n, bands):
        across = pltpu.roll(strip[0], lax.rem(2 * N - 2 - 4 * p, N), 1)
        for bx in range(2):
            extra = fix[bx, pl.ds(pl.multiple_of(8 * p, 8), 8), :]
            for r in range(8):
                at = half * bx + 8 * r
                v = own_ref[p, pl.ds(at, 8), :] + jnp.where(reached, across[at : at + 8], zero)
                if r == 0:
                    v = v + jnp.where(sub < 4, extra, zero)
                elif r == 7:
                    v = v + jnp.where(sub >= 4, extra, zero)
                if bands[bx] is not None:
                    one[bands[bx], n, pl.ds(8 * r, 8), :] = v[:, :half]
                one[bands[2 + bx], n, pl.ds(8 * r, 8), :] = pltpu.roll(v, half, 1)[:, :half]

    def low_plane(p, _):
        level_one(p, p, (None, 0, 1, 2))
        return 0

    def high_plane(p, _):
        level_one(p, p - 8, (3, 4, 5, 6))
        return 0

    outs = [
        pltpu.make_async_copy(one.at[pl.ds(0, 3)], one_ref.at[pl.ds(0, 3)], sem.at[0]),
        pltpu.make_async_copy(one.at[pl.ds(3, 4)], one_ref.at[pl.ds(3, 4)], sem.at[1]),
        pltpu.make_async_copy(two, two_ref, sem.at[2]),
        pltpu.make_async_copy(three, three_ref, sem.at[3]),
        pltpu.make_async_copy(last, last_ref, sem.at[4]),
    ]
    lax.fori_loop(8, 16, high_plane, 0)
    outs[1].start()
    lax.fori_loop(0, 8, low_plane, 0)
    outs[0].start()

    for p in DEEP:
        s, d = row_lift(z2[p, pl.ds(0, EXT // 4, stride=2), :], z2[p, pl.ds(1, EXT // 4, stride=2), :])
        z3[p] = s
        deep[p, pl.ds(0, quarter), :] = s[TOP // 4 : TOP // 4 + quarter]
        deep[p, pl.ds(quarter, quarter), :] = d[TOP // 4 : TOP // 4 + quarter]
    for p in DEEP:
        s, d = row_lift(z3[p, pl.ds(0, EXT // 8, stride=2), :], z3[p, pl.ds(1, EXT // 8, stride=2), :])
        deep[p, pl.ds(half, eighth), :] = s[TOP // 8 : TOP // 8 + eighth]
        deep[p, pl.ds(half + eighth, eighth), :] = d[TOP // 8 : TOP // 8 + eighth]
    depth = half + quarter
    slots = lax.broadcasted_iota(jnp.int32, (depth, N), 1) // 32
    halo = []
    for p in range(8):
        group, slot = p // 4, p % 4
        v = jnp.where(slots == slot, deep[LEFT + group], deep[RIGHT + group])
        halo.append(pltpu.roll(v, N - 32 * (slot + 1), 1) if slot < 3 else v)
    own = jnp.concatenate([deep[p] for p in range(8)])
    out = product(own, first[OWN_DEEP], second[OWN_DEEP]) + product(
        jnp.concatenate(halo), first[HALO_DEEP], second[HALO_DEEP]
    )
    out = out.reshape(8, depth, N)

    def put(ref, last, low, high, size):
        for n in range(len(low)):
            for band, planes in ((0, low), (4, high)):
                v = planes[n]
                for j in range(4):
                    by, bx = j // 2, j % 2
                    part = v[bx * size : (bx + 1) * size, by * size : (by + 1) * size]
                    if band + j:
                        ref[band + j - 1, n] = part
                    elif last is not None:
                        last[n] = part

    low, high = mirror_lift([out[p, :half, :half] for p in range(8)])
    put(two, None, low, high, quarter)
    outs[2].start()
    low, _ = mirror_lift([out[p, half:, half:depth] for p in range(8)])
    low, high = mirror_lift(low)
    put(three, last, low, high, eighth)
    outs[3].start()
    outs[4].start()
    for copy in outs:
        copy.wait()


def transform(extended, own, first, second):
    f32 = jnp.float32
    vmem = pl.BlockSpec(memory_space=pltpu.VMEM)
    shapes = (
        (7, 8, N // 2, N // 2),
        (7, 4, N // 4, N // 4),
        (7, 2, N // 8, N // 8),
        (2, N // 8, N // 8),
    )
    return pl.pallas_call(
        transform_kernel,
        out_shape=tuple(jax.ShapeDtypeStruct(shape, f32) for shape in shapes),
        in_specs=[vmem] * 4,
        out_specs=(pl.BlockSpec(memory_space=pltpu.HBM),) * 4,
        scratch_shapes=[pltpu.VMEM(shape, f32) for shape in shapes]
        + [
            pltpu.VMEM((2, 2 * N, N), f32),
            pltpu.VMEM((2, N, N), f32),
            pltpu.VMEM((14, EXT // 2, N), f32),
            pltpu.VMEM((14, EXT // 4, N), f32),
            pltpu.VMEM((6, N, N), f32),
            pltpu.VMEM((14, N // 2 + N // 4, N), f32),
            pltpu.SemaphoreType.DMA((5,)),
        ],
        compiler_params=pltpu.CompilerParams(vmem_limit_bytes=24 << 20),
        name="transform",
    )(extended, own, first, second)


def shards(ocean_field):
    one, deep = lane_filters()
    first, second = paired(np.concatenate([one[None, :N], deep[None, :N], deep[None, N:], strip_filters(one)]))
    return transform(*exchange(ocean_field, jnp.asarray(first), jnp.asarray(second)))


def solution(mesh):
    return jax.shard_map(
        shards,
        mesh=mesh,
        in_specs=(P(None, "gx", "gy"),),
        out_specs=(
            P(None, None, "gx", "gy"),
            P(None, None, "gx", "gy"),
            P(None, None, "gx", "gy"),
            P(None, "gx", "gy"),
        ),
        check_vma=False,
    )
```

```python
import functools

import jax
import jax.numpy as jnp
import ml_dtypes
import numpy as np
from jax import lax
from jax.experimental import pallas as pl
from jax.experimental.pallas import tpu as pltpu
from jax.sharding import PartitionSpec as P

LIFT_ALPHA = -1.586134342
LIFT_BETA = -0.05298011854
LIFT_GAMMA = 0.8829110762
LIFT_DELTA = 0.4435068522
LIFT_SCALE = 1.149604398
LIFT_INVERSE = 0.869864452

MESH = pl.DeviceIdType.MESH
N = 128
HALF, QUARTER, EIGHTH = N // 2, N // 4, N // 8
PAD = 32
ROWS = N + HALF + QUARTER
SPILL = 24
BLOCKS = 160
OWN, OWN_DEEP, REACH = 0, 1, 2
HIGH2, LOW3, HIGH3 = 40, 96, 112


def lift_matrix(extent):
    v = np.eye(extent)
    s, d = v[0::2], v[1::2]
    d = d + LIFT_ALPHA * (s + np.roll(s, -1, 0))
    s = s + LIFT_BETA * (np.roll(d, 1, 0) + d)
    d = d + LIFT_GAMMA * (s + np.roll(s, -1, 0))
    s = s + LIFT_DELTA * (np.roll(d, 1, 0) + d)
    return LIFT_SCALE * s, LIFT_INVERSE * d


def lane_filters():
    low1, high1 = lift_matrix(2 * N)
    low2, high2 = lift_matrix(N)
    low3, high3 = lift_matrix(HALF)
    one = np.concatenate([low1[:HALF], high1[:HALF]]).T
    deep = np.zeros((2 * N, N))
    deep[:, :QUARTER] = (low2 @ low1)[:QUARTER].T
    deep[:, HIGH2 : HIGH2 + QUARTER] = (high2 @ low1)[:QUARTER].T
    deep[:, LOW3:HIGH3] = (low3 @ low2 @ low1)[:EIGHTH].T
    deep[:, HIGH3:] = (high3 @ low2 @ low1)[:EIGHTH].T
    reach = np.zeros((6, N, N))
    for level, (filters, count, stride, columns) in enumerate(
        (
            (one, 16, 4, (0, 1, 62, 63, 64, 126, 127)),
            (deep, 8, 16, columns_two()),
            (deep, 4, 32, columns_three()),
        )
    ):
        wide = N // count
        for p in range(count):
            after = (p + 1) % count
            for column in columns:
                to = (column + stride * p + (2 if level == 0 else 0)) % N
                reach[2 * level, p * wide : (p + 1) * wide, to] = filters[2 * N - wide :, column]
                reach[2 * level + 1, after * wide : (after + 1) * wide, to] = filters[N : N + wide, column]
    return np.concatenate([one[None, :N], deep[None, :N], reach])


def columns_two():
    return (0, 1, 2, 29, 30, 31) + tuple(HIGH2 + c for c in (0, 1, 29, 30, 31))


def columns_three():
    return tuple(LOW3 + c for c in (0, 1, 2, 3, 13, 14, 15, 16, 17, 18, 29, 30, 31))


def parts(values, kind):
    high = values.astype(kind)
    rest = values - high.astype(values.dtype)
    middle = rest.astype(kind)
    return high, middle, (rest - middle.astype(values.dtype)).astype(kind)


def paired(weights):
    high, middle, low = parts(weights, ml_dtypes.bfloat16)
    first = np.concatenate([np.concatenate([high, middle], -1), np.concatenate([middle, high], -1)], -2)
    return first, np.concatenate([low, high], -2)


def product(values, first, second):
    high, middle, low = parts(values, jnp.bfloat16)
    wide = jnp.dot(jnp.concatenate([high, middle], axis=1), first, preferred_element_type=jnp.float32)
    rest = jnp.dot(jnp.concatenate([high, low], axis=1), second, preferred_element_type=jnp.float32)
    return wide[:, :N] + (wide[:, N:] + rest)


def mirror_lift(planes):
    count = len(planes) // 2
    s, d = list(planes[0::2]), list(planes[1::2])
    after = lambda v, n: v[min(n + 1, count - 1)]
    before = lambda v, n: v[max(n - 1, 0)]
    d = [d[n] + LIFT_ALPHA * (s[n] + after(s, n)) for n in range(count)]
    s = [s[n] + LIFT_BETA * (before(d, n) + d[n]) for n in range(count)]
    d = [d[n] + LIFT_GAMMA * (s[n] + after(s, n)) for n in range(count)]
    s = [s[n] + LIFT_DELTA * (before(d, n) + d[n]) for n in range(count)]
    return [v * LIFT_SCALE for v in s], [v * LIFT_INVERSE for v in d]


def row_lift(s, d):
    rows = s.shape[0]
    after = lambda v: pltpu.roll(v, rows - 1, 0)
    before = lambda v: pltpu.roll(v, 1, 0)
    d = d + LIFT_ALPHA * (s + after(s))
    s = s + LIFT_BETA * (before(d) + d)
    d = d + LIFT_GAMMA * (s + after(s))
    s = s + LIFT_DELTA * (before(d) + d)
    return s * LIFT_SCALE, d * LIFT_INVERSE


def exchange_kernel(
    x_ref, first_ref, second_ref, own1, own2, own3, xr, yr, first, second,
    field, padded, r1, r2, r3, z2, z3, xs, ys, load_sem, send_sem, recv_sem,
):
    nx, ny = lax.axis_size("gx"), lax.axis_size("gy")
    gx, gy = lax.axis_index("gx"), lax.axis_index("gy")
    up, down = lax.rem(gx + nx - 1, nx), lax.rem(gx + 1, nx)
    left, right = lax.rem(gy + ny - 1, ny), lax.rem(gy + 1, ny)
    barrier = pltpu.get_barrier_semaphore()
    around = [(up, gy), (down, gy), (gx, left), (gx, right), (up, left), (up, right), (down, left), (down, right)]
    for device in around:
        pl.semaphore_signal(barrier, inc=1, device_id=device, device_id_type=MESH)

    chunk = N // 4
    loads = []
    for c in range(4):
        rows = pl.ds(c * chunk, chunk)
        loads.append(pltpu.make_async_copy(x_ref.at[:, rows], field.at[:, rows], load_sem.at[c]))
        loads[-1].start()
    weights = [
        pltpu.make_async_copy(first_ref, first, load_sem.at[4]),
        pltpu.make_async_copy(second_ref, second, load_sem.at[5]),
    ]
    for copy in weights:
        copy.start()

    edge = jnp.zeros((16, PAD, N), jnp.float32)
    padded[:, pl.ds(0, PAD), :] = edge
    padded[:, pl.ds(PAD + N, PAD), :] = edge
    for array, rows, edges in ((z2, HALF + 64, 24), (z3, QUARTER + 32, 8)):
        edge = jnp.zeros((array.shape[0], edges, N), jnp.float32)
        array[:, pl.ds(0, edges), :] = edge
        array[:, pl.ds(rows - edges, edges), :] = edge

    def depth(i, _):
        at = pl.multiple_of(i * 8, 8)
        low, high = mirror_lift([field[z, pl.ds(at, 8), :] for z in range(16)])
        for n in range(8):
            padded[n, pl.ds(at + PAD, 8), :] = low[n]
            padded[8 + n, pl.ds(at + PAD, 8), :] = high[n]
        return 0

    for c in range(4):
        loads[c].wait()
        lax.fori_loop(c * 4, c * 4 + 4, depth, 0, unroll=2)

    def spills(s, d, begin, end, shift_up, shift_down):
        over = s[begin - 8 : begin] + pltpu.roll(d[begin - 8 : begin], 8 - shift_up, 0)
        under = s[end : end + 8] + pltpu.roll(d[end : end + 8], shift_down, 0)
        return over, under

    def rows_one(p, _):
        both = []
        for q in (p, p + 8):
            s, d = row_lift(padded[q, pl.ds(0, 96, stride=2), :], padded[q, pl.ds(1, 96, stride=2), :])
            r1[q, pl.ds(0, HALF), :] = s[16 : 16 + HALF]
            r1[q, pl.ds(HALF, HALF), :] = d[16 : 16 + HALF]
            over, under = spills(s, d, 16, 80, 2, 2)
            r1[q, pl.ds(N, 8), :] = over
            r1[q, pl.ds(N + 8, 8), :] = under
            both.append((over, under))
            if q is p:
                z2[p, pl.ds(24, 80), :] = s[8:88]
        at = pl.ds(pl.multiple_of(8 * p, 8), 8)
        for way in range(2):
            xs[way, at, :] = both[0][way] + pltpu.roll(both[1][way], 4, 0)
        return 0

    lax.fori_loop(0, 8, rows_one, 0)

    def depth_two(i, _):
        at = pl.ds(pl.multiple_of(24 + 8 * i, 8), 8)
        low, high = mirror_lift([z2[p, at, :] for p in range(8)])
        for n in range(4):
            z2[n, at, :] = low[n]
            z2[4 + n, at, :] = high[n]
        return 0

    lax.fori_loop(0, 10, depth_two, 0, unroll=2)
    for p in range(8):
        s, d = row_lift(z2[p, pl.ds(0, 64, stride=2), :], z2[p, pl.ds(1, 64, stride=2), :])
        r2[p, pl.ds(0, QUARTER), :] = s[16 : 16 + QUARTER]
        r2[p, pl.ds(QUARTER, QUARTER), :] = d[16 : 16 + QUARTER]
        for way, part in enumerate(spills(s, d, 16, 48, 3, 3)):
            r2[p, pl.ds(HALF + 8 * way, 8), :] = part
            xs[way, pl.ds(HALF + 8 * p, 8), :] = part
        if p < 4:
            z3[p, pl.ds(8, 48), :] = s[8:56]
    for i in range(6):
        at = pl.ds(8 + 8 * i, 8)
        low, high = mirror_lift([z3[p, at, :] for p in range(4)])
        for n in range(2):
            z3[n, at, :] = low[n]
            z3[2 + n, at, :] = high[n]
    for p in range(4):
        s, d = row_lift(z3[p, pl.ds(0, 32, stride=2), :], z3[p, pl.ds(1, 32, stride=2), :])
        r3[p, pl.ds(0, EIGHTH), :] = s[8 : 8 + EIGHTH]
        r3[p, pl.ds(EIGHTH, EIGHTH), :] = d[8 : 8 + EIGHTH]
        for way, part in enumerate(spills(s, d, 8, 24, 3, 4)):
            r3[p, pl.ds(QUARTER + 8 * way, 8), :] = part
            xs[way, pl.ds(N + 8 * p, 8), :] = part

    lane = lax.broadcasted_iota(jnp.int32, (8, N), 1)

    def pack(r, at, to):
        count = r.shape[0]
        wide = N // count
        slot = lane // wide
        to_right, to_left = None, None
        for j in range(count):
            v = r[j, at, :]
            turned = pltpu.roll(v, wide * (j + 1), 1) if j < count - 1 else v
            to_right = turned if j == 0 else jnp.where(slot == j, turned, to_right)
            to_left = turned if j == 0 else jnp.where(slot == (j + 1) % count, turned, to_left)
        ys[0, to, :] = to_right
        ys[1, to, :] = to_left

    def packs(i, _):
        at = pl.ds(pl.multiple_of(8 * i, 8), 8)
        pack(r1, at, at)
        return 0

    lax.fori_loop(0, 16, packs, 0, unroll=2)
    for i in range(8):
        pack(r2, pl.ds(8 * i, 8), pl.ds(N + 8 * i, 8))
    for i in range(4):
        pack(r3, pl.ds(8 * i, 8), pl.ds(N + HALF + 8 * i, 8))
    for way in range(2):
        for level, (r, rows) in enumerate(((r1, N), (r2, HALF), (r3, QUARTER))):
            pack(r, pl.ds(rows + 8 * way, 8), pl.ds(ROWS + SPILL * way + 8 * level, 8))

    pl.semaphore_wait(barrier, len(around))
    own, over, under = pl.ds(0, ROWS), pl.ds(ROWS, SPILL), pl.ds(ROWS + SPILL, SPILL)
    moves = [
        (ys.at[0, under], yr.at[0, over], (down, right)),
        (ys.at[0, over], yr.at[0, under], (up, right)),
        (ys.at[1, under], yr.at[1, over], (down, left)),
        (ys.at[1, over], yr.at[1, under], (up, left)),
        (xs.at[1], xr.at[0], (down, gy)),
        (xs.at[0], xr.at[1], (up, gy)),
        (ys.at[0, own], yr.at[0, own], (gx, right)),
        (ys.at[1, own], yr.at[1, own], (gx, left)),
    ]
    copies = []
    for k, (source, target, device) in enumerate(moves):
        copies.append(
            pltpu.make_async_remote_copy(
                src_ref=source,
                dst_ref=target,
                send_sem=send_sem.at[k],
                recv_sem=recv_sem.at[k],
                device_id=device,
                device_id_type=MESH,
            )
        )
        copies[-1].start()

    for copy in weights:
        copy.wait()

    def plane(p, _):
        own1[p] = product(r1[p, pl.ds(0, N), :], first[OWN], second[OWN])
        return 0

    lax.fori_loop(0, 16, plane, 0)

    def deeper(p, _):
        own2[p] = product(r2[p, pl.ds(0, HALF), :], first[OWN_DEEP], second[OWN_DEEP])
        return 0

    lax.fori_loop(0, 8, deeper, 0)
    out = product(
        jnp.concatenate([r3[p, pl.ds(0, QUARTER), :] for p in range(4)]), first[OWN_DEEP], second[OWN_DEEP]
    )
    own3[...] = out.reshape(4, QUARTER, N)
    for copy in copies:
        copy.wait_recv()
    for copy in copies:
        copy.wait_send()


def exchange(field, first, second):
    f32 = jnp.float32
    shapes = ((16, N, N), (8, HALF, N), (4, QUARTER, N), (2, BLOCKS, N), (2, ROWS + 2 * SPILL, N))
    outs = [jax.ShapeDtypeStruct(shape, f32) for shape in shapes]
    outs += [jax.ShapeDtypeStruct(v.shape, v.dtype) for v in (first, second)]
    return pl.pallas_call(
        exchange_kernel,
        out_shape=tuple(outs),
        in_specs=[pl.BlockSpec(memory_space=pltpu.HBM)] * 3,
        out_specs=(pl.BlockSpec(memory_space=pltpu.VMEM),) * len(outs),
        scratch_shapes=[
            pltpu.VMEM((16, N, N), f32),
            pltpu.VMEM((16, N + 2 * PAD, N), f32),
            pltpu.VMEM((16, N + 16, N), f32),
            pltpu.VMEM((8, HALF + 16, N), f32),
            pltpu.VMEM((4, QUARTER + 16, N), f32),
            pltpu.VMEM((8, N, N), f32),
            pltpu.VMEM((4, HALF, N), f32),
            pltpu.VMEM((2, BLOCKS, N), f32),
            pltpu.VMEM((2, ROWS + 2 * SPILL, N), f32),
            pltpu.SemaphoreType.DMA((6,)),
            pltpu.SemaphoreType.DMA((8,)),
            pltpu.SemaphoreType.DMA((8,)),
        ],
        compiler_params=pltpu.CompilerParams(collective_id=0, has_side_effects=True, vmem_limit_bytes=20 << 20),
        name="exchange",
    )(*[pltpu.with_memory_space_constraint(v, pltpu.HBM) for v in (field, first, second)])


def transform_kernel(
    own1, own2, own3, xr, yr, first, second,
    one_ref, two_ref, three_ref, last_ref, one, two, three, last, fix, across, sem,
):
    f32 = jnp.float32
    sub = lax.broadcasted_iota(jnp.int32, (8, N), 0)
    lane = lax.broadcasted_iota(jnp.int32, (8, N), 1)
    zero = jnp.zeros((8, N), f32)

    def landed(level, over, under):
        low, high, back = ((2, 1, 2), (3, 2, 3), (4, 3, 3))[level]
        return (
            jnp.where(sub < low, over, zero),
            jnp.where(sub >= 8 - back, under, zero),
            jnp.where(sub < high, pltpu.roll(over, 8 - low, 0), zero),
            jnp.where(sub >= 8 - back, pltpu.roll(under, back, 0), zero),
        )

    at = 0
    for level, rows in enumerate((N, HALF, QUARTER)):
        total = None
        for way in range(2):
            over, under = yr[way, pl.ds(ROWS + 8 * level, 8), :], yr[way, pl.ds(ROWS + SPILL + 8 * level, 8), :]
            parts_in = landed(level, over, under)
            pieces, places = [], (0, rows // 2 - 8, rows // 2, rows - 8)
            for r in range(0, rows, 8):
                pieces.append(yr[way, pl.ds(at + r, 8), :])
                for k, place in enumerate(places):
                    if r == place:
                        pieces[-1] = pieces[-1] + parts_in[k]
            weight = REACH + 2 * level + way
            out = product(jnp.concatenate(pieces), first[weight], second[weight])
            total = out if total is None else total + out
        across[pl.ds(at, rows), :] = total
        at += rows
    for way in range(2):
        fix[way, pl.ds(0, HALF), :] = product(xr[way, pl.ds(0, HALF), :], first[OWN], second[OWN])
        fix[way, pl.ds(HALF, BLOCKS - HALF), :] = product(
            xr[way, pl.ds(HALF, BLOCKS - HALF), :], first[OWN_DEEP], second[OWN_DEEP]
        )

    def reached(columns):
        hit = lane == columns[0]
        for column in columns[1:]:
            hit = hit | (lane == column)
        return hit

    def finish(level, own, turned, hit, parts_in, rows, store):
        for k in range(rows // 8):
            v = own(8 * k) + jnp.where(hit, turned[8 * k : 8 * k + 8], zero)
            for part, place in zip(parts_in, (0, rows // 16 - 1, rows // 16, rows // 8 - 1)):
                if k == place:
                    v = v + part
            bx, r = divmod(8 * k, rows // 2)
            store(bx, r, v)

    hit1 = (lane < 2) | (lane >= N - 2) | ((lane >= HALF - 2) & (lane <= HALF))

    def level_one(p, n, turn, bands):
        turned = pltpu.roll(across[pl.ds(0, N), :], lax.rem(2 * N - 2 - 4 * p, N), 1)
        at = pl.ds(pl.multiple_of(8 * n, 8), 8)
        over, under = fix[0, at, :], fix[1, at, :]
        if turn:
            over, under = pltpu.roll(over, 4, 0), pltpu.roll(under, 4, 0)

        def store(bx, r, v):
            if bands[bx] is not None:
                one[bands[bx], n, pl.ds(r, 8), :] = v[:, :HALF]
            one[bands[2 + bx], n, pl.ds(r, 8), :] = pltpu.roll(v, HALF, 1)[:, :HALF]

        finish(0, lambda at: own1[p, pl.ds(at, 8), :], turned, hit1, landed(0, over, under), N, store)

    def low_plane(n, _):
        level_one(n, n, False, (None, 0, 1, 2))
        return 0

    def high_plane(n, _):
        level_one(n + 8, n, True, (3, 4, 5, 6))
        return 0

    outs = [
        pltpu.make_async_copy(one.at[pl.ds(0, 3)], one_ref.at[pl.ds(0, 3)], sem.at[0]),
        pltpu.make_async_copy(one.at[pl.ds(3, 4)], one_ref.at[pl.ds(3, 4)], sem.at[1]),
        pltpu.make_async_copy(two, two_ref, sem.at[2]),
        pltpu.make_async_copy(three, three_ref, sem.at[3]),
        pltpu.make_async_copy(last, last_ref, sem.at[4]),
    ]
    lax.fori_loop(0, 8, high_plane, 0)
    outs[1].start()
    lax.fori_loop(0, 8, low_plane, 0)
    outs[0].start()

    def deeper(level, count, rows, at, block, own, columns, bases, size, out, corner):
        hit = reached(columns)
        wide = N // count
        for p in range(count):
            turned = across[pl.ds(at, rows), :]
            if p:
                turned = pltpu.roll(turned, N - wide * p, 1)
            here = pl.ds(block + 8 * p, 8)
            bz, n = divmod(p, count // 2)

            def store(bx, r, v):
                for by in range(2):
                    band = 4 * bz + 2 * by + bx
                    part = v[:, bases[by] : bases[by] + size]
                    if band:
                        out[band - 1, n, pl.ds(r, 8), :] = part
                    elif corner is not None:
                        corner[n, pl.ds(r, 8), :] = part

            finish(level, lambda at: own[p, pl.ds(at, 8), :], turned, hit, landed(level, fix[0, here, :], fix[1, here, :]), rows, store)

    deeper(1, 8, HALF, N, HALF, own2, columns_two(), (0, HIGH2), QUARTER, two, None)
    outs[2].start()
    deeper(2, 4, QUARTER, N + HALF, N, own3, columns_three(), (LOW3, HIGH3), EIGHTH, three, last)
    outs[3].start()
    outs[4].start()
    for copy in outs:
        copy.wait()


def transform(*arrays):
    f32 = jnp.float32
    shapes = ((7, 8, HALF, HALF), (7, 4, QUARTER, QUARTER), (7, 2, EIGHTH, EIGHTH), (2, EIGHTH, EIGHTH))
    return pl.pallas_call(
        transform_kernel,
        out_shape=tuple(jax.ShapeDtypeStruct(shape, f32) for shape in shapes),
        in_specs=[pl.BlockSpec(memory_space=pltpu.VMEM)] * len(arrays),
        out_specs=(pl.BlockSpec(memory_space=pltpu.HBM),) * 4,
        scratch_shapes=[pltpu.VMEM(shape, f32) for shape in shapes]
        + [
            pltpu.VMEM((2, BLOCKS, N), f32),
            pltpu.VMEM((ROWS, N), f32),
            pltpu.SemaphoreType.DMA((5,)),
        ],
        compiler_params=pltpu.CompilerParams(vmem_limit_bytes=20 << 20),
        name="transform",
    )(*arrays)


def shards(ocean_field):
    first, second = paired(lane_filters())
    return transform(*exchange(ocean_field, jnp.asarray(first), jnp.asarray(second)))


def solution(mesh):
    return jax.shard_map(
        shards,
        mesh=mesh,
        in_specs=(P(None, "gx", "gy"),),
        out_specs=(
            P(None, None, "gx", "gy"),
            P(None, None, "gx", "gy"),
            P(None, None, "gx", "gy"),
            P(None, "gx", "gy"),
        ),
        check_vma=False,
    )
```
